32 devices in a mesh: expert: 8 (over z, y), blk: 4 (over x, core).
Axes of the slice: x: 2, y: 2, z: 4, core: 2. Of those that a mesh axis runs over, the one named last changes fastest.
Arguments:
- inputs: bfloat16 [8, 768, 1536], P('expert', 'blk'), may hold values from -6 to 6
- output_grads: bfloat16 [8, 768, 4096], P('expert', 'blk'), may hold values from -0.21875 to 0.21875
- route_counts: int32 [8, 4], P('expert', 'blk'), may hold values from 48 to 192, as said below
- left_rows: bfloat16 [8, 2304, 1536], P(None, 'expert', 'blk'), as said below
- left_lengths: int32 [8, 8], replicated, may hold values from 96 to 288, as said below
- right_inverse: bfloat16 [8, 4096, 4096], P('expert', 'blk'), may hold values from -0.09375 to 0.09375
Outputs:
- preconditioned: float32 [8, 4096, 1536], P('expert', 'blk')
The draws below stay inside these ranges and needn't reach their ends.
Inputs may be any that keep to these rules, and one draw needn't show every extreme that they name: `route_counts`: for every expert, one device of blk holds exactly 192 routed tokens and one holds exactly 48. `left_lengths`: each row sums to 1536; in each row one owner holds exactly 288 rows and one exactly 96. `left_rows`: slots i * 288 + j with j >= left_lengths[e, i] are zero.
All inputs are finite; a program needn't handle non-finite values.
Results may differ from the reference program's by a relative error of at most 0.0041.
Values may be sent and summed in bfloat16 or wider, within the bound.
A program may use at most 128 MiB of HBM per device.

```python
import math
import jax
import jax.numpy as jnp
from jax import lax

D = 4096
F = 1536
CAP = 192
EXPERTS = 8
OWNERS = 8
GROUP = 4
SHARE = 192
PR = 288


def piece_lengths(key):
    base_key = jax.random.fold_in(key, 11)
    expert_keys = jax.random.split(base_key, EXPERTS)

    def one_row(row_key):
        order_key, moves_key = jax.random.split(row_key)
        order = jax.random.permutation(order_key, OWNERS)
        reach = PR - SHARE
        moves = jax.random.randint(moves_key, (OWNERS // 2,), -reach, reach + 1)
        moves = moves.at[0].set(reach)
        paired = jnp.stack([SHARE + moves, SHARE - moves], axis=1).reshape(OWNERS).astype(jnp.int32)
        return jnp.zeros((OWNERS,), jnp.int32).at[order].set(paired)
    return jax.vmap(one_row)(expert_keys)


def draw_left_lengths(key, part):
    return piece_lengths(key)


def draw_left_rows(key, part):
    lengths = piece_lengths(key)
    float_key = jax.random.fold_in(key, 23)
    noise = jax.random.normal(float_key, (EXPERTS, F, F), jnp.float32)
    factor = jnp.eye(F, dtype=jnp.float32)[None] + 0.5 / math.sqrt(F) * noise
    starts = jnp.cumsum(lengths, axis=1) - lengths
    slot_pos = jnp.arange(PR, dtype=jnp.int32)
    row_index = jnp.minimum(starts[:, :, None] + slot_pos[None, None, :], F - 1).reshape(EXPERTS, OWNERS * PR)
    kept_rows = (slot_pos[None, None, :] < lengths[:, :, None]).reshape(EXPERTS, OWNERS * PR, 1)
    picked = jnp.take_along_axis(factor, row_index[:, :, None], axis=1)
    return jnp.where(kept_rows, picked, 0.0).astype(jnp.bfloat16)


def draw_route_counts(key, part):
    span = CAP - CAP // 4
    first_key, second_key, order_key = jax.random.split(key, 3)
    first = jax.random.randint(first_key, (EXPERTS, GROUP), 0, span + 1)
    second = jax.random.randint(second_key, (EXPERTS, GROUP), 0, span + 1)
    counts = CAP - first * second // span
    order = jax.vmap(lambda row_key: jax.random.permutation(row_key, GROUP))(jax.random.split(order_key, EXPERTS))
    counts = jnp.where(order == 0, CAP, counts)
    counts = jnp.where(order == 1, CAP // 4, counts)
    return counts.astype(jnp.int32)


def block_levels(rng, shape, cuts, least, largest):
    gain = 1.0
    for axis_at, blocks in cuts:
        draws = jax.random.uniform(jax.random.fold_in(jax.random.fold_in(rng, 6), axis_at), (blocks,), jnp.float32, least / len(cuts), largest / len(cuts))
        gain = gain * jnp.repeat(jnp.exp(draws), shape[axis_at] // blocks).reshape((-1,) + (1,) * (len(shape) - 1 - axis_at))
    return gain


def normal_values(own_key, extent, spread, most, cuts=(), kind=jnp.bfloat16):
    result = jax.random.normal(own_key, extent, jnp.float32) * spread
    if len(cuts) > 0:
        result = block_levels(own_key, extent, cuts, -0.22, 0.18) * result
    return jnp.clip(result, min=-most, max=most).astype(kind)


def setup_inputs(seed: int = 0) -> dict:
    seeds = jax.random.split(jax.random.key(seed), 7)
    inputs = normal_values(seeds[0], (EXPERTS, GROUP * CAP, F), 1.0, 6.0, ((0, 8), (1, 4)))
    output_grads = normal_values(seeds[1], (EXPERTS, GROUP * CAP, D), (GROUP * CAP) ** -0.5, 0.21875, ((0, 8), (1, 4)))
    route_counts = draw_route_counts(jax.random.fold_in(seeds[6], 71), 0)
    left_rows = draw_left_rows(jax.random.fold_in(seeds[6], 71), 0)
    left_lengths = draw_left_lengths(jax.random.fold_in(seeds[6], 71), 0)
    right_inverse = normal_values(seeds[5], (EXPERTS, D, D), D ** -0.5, 0.09375, ((0, 8), (1, 4)))
    return {"inputs": inputs, "output_grads": output_grads, "route_counts": route_counts, "left_rows": left_rows, "left_lengths": left_lengths, "right_inverse": right_inverse}


def one_expert(operands):
    rows_in, grads_out, counts, pieces, lengths, inverse_right = operands
    slot_pos = lax.broadcasted_iota(jnp.int32, (GROUP, CAP), 1)
    live_rows = (slot_pos < counts[:, None]).reshape(GROUP * CAP, 1)
    masked = jnp.where(live_rows, rows_in, jnp.zeros_like(rows_in))
    gradient = lax.dot_general(grads_out, masked, (((0,), (0,)), ((), ())), preferred_element_type=jnp.float32).astype(jnp.bfloat16)
    starts = jnp.cumsum(lengths) - lengths
    offset = lax.broadcasted_iota(jnp.int32, (OWNERS, PR), 1)
    row_index = jnp.minimum(starts[:, None] + offset, F - 1).reshape(OWNERS * PR).astype(jnp.int32)
    kept_rows = (offset < lengths[:, None]).reshape(OWNERS * PR, 1)
    values = jnp.where(kept_rows, pieces.astype(jnp.float32), jnp.zeros((), jnp.float32))
    factor = jnp.zeros((F, F), jnp.float32).at[row_index].add(values).astype(jnp.bfloat16)
    weighted = jnp.dot(gradient, factor, preferred_element_type=jnp.float32).astype(jnp.bfloat16)
    return jnp.dot(inverse_right, weighted, preferred_element_type=jnp.float32)


def reference(inputs, output_grads, route_counts, left_rows, left_lengths, right_inverse):
    return lax.map(one_expert, (inputs, output_grads, route_counts, left_rows, left_lengths, right_inverse))
```

```python
import jax
import jax.numpy as jnp
from jax import lax
from jax.sharding import PartitionSpec as P


def shards(inputs, output_grads, route_counts, left_rows, left_lengths, right_inverse):
    token_rows = inputs[0]
    slot_count, width_in = token_rows.shape
    owners, piece_slots = left_lengths.shape[1], left_rows.shape[1]
    live_rows = lax.broadcasted_iota(jnp.int32, (slot_count, 1), 0) < route_counts[0, 0]
    masked = jnp.where(live_rows, token_rows, jnp.zeros_like(token_rows))
    tokens = lax.all_gather(masked, "blk", axis=0, tiled=True)
    grads = lax.all_gather(output_grads[0], "blk", axis=0, tiled=True)
    arrived = lax.all_to_all(left_rows, "expert", split_axis=0, concat_axis=1, tiled=True)[0]

    lengths = lax.dynamic_index_in_dim(left_lengths, lax.axis_index("expert"), 0, keepdims=False)
    starts = jnp.cumsum(lengths) - lengths
    offset = lax.broadcasted_iota(jnp.int32, (owners, piece_slots), 1)
    row_index = jnp.where(offset < lengths[:, None], starts[:, None] + offset, -1)
    row_index = row_index.reshape(1, owners * piece_slots)
    select = lax.broadcasted_iota(jnp.int32, (width_in, 1), 0) == row_index
    picked = jnp.dot(tokens, select.astype(jnp.bfloat16), preferred_element_type=jnp.float32)
    picked = picked.astype(jnp.bfloat16)
    mixed = lax.dot_general(
        arrived, picked, (((0,), (1,)), ((), ())), preferred_element_type=jnp.float32
    ).astype(jnp.bfloat16)
    mixed = lax.all_gather(mixed, "blk", axis=0, tiled=True)

    trans_b = (((1,), (1,)), ((), ()))
    scores = lax.dot_general(
        right_inverse[0], grads, trans_b, preferred_element_type=jnp.float32
    ).astype(jnp.bfloat16)
    result = lax.dot_general(scores, mixed, trans_b, preferred_element_type=jnp.float32)
    return result[None]


def solution(mesh):
    in_specs = (
        P("expert", "blk", None),
        P("expert", "blk", None),
        P("expert", "blk"),
        P(None, "expert", "blk"),
        P(),
        P("expert", "blk", None),
    )
    out_specs = P("expert", "blk", None)
    return jax.shard_map(shards, mesh=mesh, in_specs=in_specs, out_specs=out_specs, check_vma=False)
```

```python
import functools

import jax
import jax.numpy as jnp
from jax import lax
from jax.experimental import pallas as pl
from jax.experimental.pallas import tpu as pltpu
from jax.sharding import PartitionSpec as P

MESH = pl.DeviceIdType.MESH
GRAD_PARTS = 4
MIX_PARTS = 2


def gather_kernel(
    experts, group, x_ref, dy_ref, count_ref, pieces_ref, lengths_ref, right_ref,
    scores_ref, mixed_ref,
    x_own, x_all, dy_all, right, arrived, picked, mix_own, scores,
    local_sem, send_sem, recv_sem,
):
    expert, block = lax.axis_index("expert"), lax.axis_index("blk")
    mate = block + 1 - 2 * (block % 2)
    across = (block + 2) % group
    corner = (mate + 2) % group
    slots, width_in = x_ref.shape
    width_out = dy_ref.shape[1]
    owners, piece, columns = pieces_ref.shape
    tokens = slots * group
    own_rows = right_ref.shape[0]

    numbers = iter(range(1000))
    local_numbers = iter(range(1000))

    def rows_of(source, part=0, parts=1):
        size = slots // parts
        return pl.ds(pl.multiple_of(source * slots + part * size, 16), size)

    def local(source, target):
        copy = pltpu.make_async_copy(source, target, local_sem.at[next(local_numbers)])
        copy.start()
        return copy

    def remote(source, target, number, device):
        return pltpu.make_async_remote_copy(
            src_ref=source, dst_ref=target, send_sem=send_sem.at[number],
            recv_sem=recv_sem.at[number], device_id=device, device_id_type=MESH,
        )

    sent = []

    def send(source, target, number, device):
        copy = remote(source, target, number, device)
        copy.start()
        sent.append(copy)

    def receive(target, number, device):
        remote(target, target, number, device).wait_recv()

    to_mate, to_across = (expert, mate), (expert, across)

    x_load = local(x_ref, x_own)
    dy_load = local(dy_ref, dy_all.at[rows_of(block)])
    right_load = local(right_ref, right)
    piece_rows = lambda owner: pl.ds(pl.multiple_of(owner * piece, 16), piece)
    piece_load = local(pieces_ref.at[expert], arrived.at[piece_rows(expert)])

    shifts = sorted(range(1, experts), key=lambda k: abs(k - experts / 2))
    barrier = pltpu.get_barrier_semaphore()
    for shift in shifts:
        pl.semaphore_signal(
            barrier, inc=1, device_id=((expert + shift) % experts, block), device_id_type=MESH
        )
    for device in (to_mate, to_across):
        pl.semaphore_signal(barrier, inc=1, device_id=device, device_id_type=MESH)
    pl.semaphore_wait(barrier, experts + 1)

    piece_numbers = []
    for shift in shifts:
        number = next(numbers)
        piece_numbers.append(number)
        target = (expert + shift) % experts
        send(pieces_ref.at[target], arrived.at[piece_rows(expert)], number, (target, block))

    x_load.wait()
    live = lax.broadcasted_iota(jnp.int32, (slots, 1), 0) < count_ref[0, 0]
    x_all[rows_of(block), :] = jnp.where(
        live, x_own[...].astype(jnp.float32), 0.0
    ).astype(jnp.bfloat16)
    x_mate, x_across, x_pass = next(numbers), next(numbers), next(numbers)
    own = x_all.at[rows_of(block)]
    send(own, own, x_across, to_across)
    send(own, own, x_mate, to_mate)

    dy_mate = next(numbers)
    dy_across = [next(numbers) for _ in range(GRAD_PARTS)]
    dy_pass = [next(numbers) for _ in range(GRAD_PARTS)]
    for part, number in enumerate(dy_across):
        size = slots // GRAD_PARTS
        send(
            dy_ref.at[pl.ds(part * size, size)],
            dy_all.at[rows_of(block, part, GRAD_PARTS)], number, to_across,
        )
    send(dy_ref, dy_all.at[rows_of(block)], dy_mate, to_mate)

    receive(x_all.at[rows_of(across)], x_across, to_across)
    send(x_all.at[rows_of(across)], x_all.at[rows_of(across)], x_pass, to_mate)
    receive(x_all.at[rows_of(mate)], x_mate, to_mate)

    trans_b = (((1,), (1,)), ((), ()))
    pair_width = 2 * slots
    tile = min(256, own_rows)

    def score(pair):
        rows = pl.ds(pl.multiple_of(pair * pair_width, 128), pair_width)

        @pl.loop(0, own_rows // tile)
        def _(step):
            here = pl.ds(pl.multiple_of(step * tile, tile), tile)
            scores[here, rows] = lax.dot_general(
                right[here, :], dy_all[rows, :], trans_b, preferred_element_type=jnp.float32
            ).astype(jnp.bfloat16)

    receive(x_all.at[rows_of(corner)], x_pass, to_mate)

    lengths = [lengths_ref[expert, i] for i in range(owners)]
    starts = [jnp.int32(0)]
    for length in lengths[:-1]:
        starts.append(starts[-1] + length)
    wide = 256

    @pl.loop(0, owners * piece // wide)
    def _(step):
        slot = lax.broadcasted_iota(jnp.int32, (1, wide), 1) + step * wide
        index = jnp.full((1, wide), -1, jnp.int32)
        for i in range(owners):
            offset = slot - i * piece
            index = jnp.where((offset >= 0) & (offset < lengths[i]), starts[i] + offset, index)
        select = lax.broadcasted_iota(jnp.int32, (width_in, wide), 0) == index
        select = jnp.where(select, 1.0, 0.0).astype(jnp.bfloat16)
        picked[:, pl.ds(pl.multiple_of(step * wide, wide), wide)] = jnp.dot(
            x_all[...], select, preferred_element_type=jnp.float32
        ).astype(jnp.bfloat16)

    dy_load.wait()
    right_load.wait()
    receive(dy_all.at[rows_of(mate)], dy_mate, to_mate)
    score(block // 2)

    def pass_grads(part):
        here = dy_all.at[rows_of(across, part, GRAD_PARTS)]
        receive(here, dy_across[part], to_across)
        send(here, here, dy_pass[part], to_mate)

    for part in range(GRAD_PARTS - 1):
        pass_grads(part)

    piece_load.wait()
    for shift, number in zip(shifts, piece_numbers):
        source = (expert + experts - shift) % experts
        receive(arrived.at[piece_rows(source)], number, (source, block))

    mix_size = tokens // MIX_PARTS
    mix_mate = [next(numbers) for _ in range(MIX_PARTS)]
    mix_across = [next(numbers) for _ in range(MIX_PARTS)]
    mix_pass = [next(numbers) for _ in range(MIX_PARTS)]
    mix_keep = []

    def mix_at(source, part):
        lanes = pl.ds(pl.multiple_of(source * columns, 128), columns)
        return mixed_ref.at[pl.ds(part * mix_size, mix_size), lanes]

    for part in range(MIX_PARTS):
        here = pl.ds(part * mix_size, mix_size)
        mix_own[here, :] = jnp.dot(
            picked[here, :], arrived[...], preferred_element_type=jnp.float32
        ).astype(jnp.bfloat16)
        send(mix_own.at[here], mix_at(block, part), mix_across[part], to_across)
        send(mix_own.at[here], mix_at(block, part), mix_mate[part], to_mate)
        mix_keep.append(local(mix_own.at[here], mix_at(block, part)))

    pass_grads(GRAD_PARTS - 1)
    for part in range(GRAD_PARTS):
        receive(dy_all.at[rows_of(corner, part, GRAD_PARTS)], dy_pass[part], to_mate)
    score(1 - block // 2)
    scores_keep = local(scores, scores_ref)

    for part in range(MIX_PARTS):
        receive(mix_at(across, part), mix_across[part], to_across)
        send(mix_at(across, part), mix_at(across, part), mix_pass[part], to_mate)
    for part in range(MIX_PARTS):
        receive(mix_at(mate, part), mix_mate[part], to_mate)
    for part in range(MIX_PARTS):
        receive(mix_at(corner, part), mix_pass[part], to_mate)
    for copy in mix_keep:
        copy.wait()
    scores_keep.wait()
    for copy in sent:
        copy.wait_send()


def paired(experts, group, inputs, output_grads, route_counts, left_rows, left_lengths, right_inverse):
    slots, width_in = inputs.shape[1:]
    width_out = output_grads.shape[2]
    owners, piece, columns = left_rows.shape
    own_rows = right_inverse.shape[1]
    tokens = group * slots
    copies = experts - 1 + 4 + 2 * GRAD_PARTS + 3 * MIX_PARTS
    any_space = pl.BlockSpec(memory_space=pl.ANY)
    scalars = pl.BlockSpec(memory_space=pltpu.SMEM)
    bf16 = jnp.bfloat16
    scores, mixed = pl.pallas_call(
        functools.partial(gather_kernel, experts, group),
        name="exchange",
        out_shape=(
            jax.ShapeDtypeStruct((own_rows, tokens), bf16),
            jax.ShapeDtypeStruct((tokens, width_in), bf16),
        ),
        in_specs=[any_space, any_space, scalars, any_space, scalars, any_space],
        out_specs=(any_space, any_space),
        scratch_shapes=[
            pltpu.VMEM((slots, width_in), bf16),
            pltpu.VMEM((tokens, width_in), bf16),
            pltpu.VMEM((tokens, width_out), bf16),
            pltpu.VMEM((own_rows, width_out), bf16),
            pltpu.VMEM((owners * piece, columns), bf16),
            pltpu.VMEM((tokens, owners * piece), bf16),
            pltpu.VMEM((tokens, columns), bf16),
            pltpu.VMEM((own_rows, tokens), bf16),
            pltpu.SemaphoreType.DMA((5 + MIX_PARTS,)),
            pltpu.SemaphoreType.DMA((copies,)),
            pltpu.SemaphoreType.DMA((copies,)),
        ],
        compiler_params=pltpu.CompilerParams(
            collective_id=0, has_side_effects=True, vmem_limit_bytes=60 * 2**20
        ),
    )(inputs[0], output_grads[0], route_counts, left_rows, left_lengths, right_inverse[0])
    return jnp.dot(scores, mixed, preferred_element_type=jnp.float32)[None]


def shards(inputs, output_grads, route_counts, left_rows, left_lengths, right_inverse):
    token_rows = inputs[0]
    slot_count, width_in = token_rows.shape
    owners, piece_slots = left_lengths.shape[1], left_rows.shape[1]
    live_rows = lax.broadcasted_iota(jnp.int32, (slot_count, 1), 0) < route_counts[0, 0]
    masked = jnp.where(live_rows, token_rows, jnp.zeros_like(token_rows))
    tokens = lax.all_gather(masked, "blk", axis=0, tiled=True)
    grads = lax.all_gather(output_grads[0], "blk", axis=0, tiled=True)
    arrived = lax.all_to_all(left_rows, "expert", split_axis=0, concat_axis=1, tiled=True)[0]

    lengths = lax.dynamic_index_in_dim(left_lengths, lax.axis_index("expert"), 0, keepdims=False)
    starts = jnp.cumsum(lengths) - lengths
    offset = lax.broadcasted_iota(jnp.int32, (owners, piece_slots), 1)
    row_index = jnp.where(offset < lengths[:, None], starts[:, None] + offset, -1)
    row_index = row_index.reshape(1, owners * piece_slots)
    select = lax.broadcasted_iota(jnp.int32, (width_in, 1), 0) == row_index
    picked = jnp.dot(tokens, select.astype(jnp.bfloat16), preferred_element_type=jnp.float32)
    picked = picked.astype(jnp.bfloat16)
    mixed = lax.dot_general(
        arrived, picked, (((0,), (1,)), ((), ())), preferred_element_type=jnp.float32
    ).astype(jnp.bfloat16)
    mixed = lax.all_gather(mixed, "blk", axis=0, tiled=True)

    trans_b = (((1,), (1,)), ((), ()))
    scores = lax.dot_general(
        right_inverse[0], grads, trans_b, preferred_element_type=jnp.float32
    ).astype(jnp.bfloat16)
    result = lax.dot_general(scores, mixed, trans_b, preferred_element_type=jnp.float32)
    return result[None]


def solution(mesh):
    in_specs = (
        P("expert", "blk", None),
        P("expert", "blk", None),
        P("expert", "blk"),
        P(None, "expert", "blk"),
        P(),
        P("expert", "blk", None),
    )
    out_specs = P("expert", "blk", None)
    experts, group = mesh.shape["expert"], mesh.shape["blk"]
    step = functools.partial(paired, experts, group) if group == 4 else shards
    return jax.shard_map(step, mesh=mesh, in_specs=in_specs, out_specs=out_specs, check_vma=False)
```
